32 devices in a mesh: row: 8 (over y, x, core), col: 4 (over z).
Axes of the slice: x: 2, y: 2, z: 4, core: 2. Of those that a mesh axis runs over, the one named last changes fastest.
Arguments:
- object_field: float32 [2, 4096, 2048], P(None, 'row', 'col'), may hold values from -6 to 6
- probe: float32 [3, 2, 256, 256], replicated, may hold values from -6 to 6
- raw_counts: bfloat16 [192, 256, 256], P(('row', 'col')), may hold values from 0.099609375 to 10
- resample_delta: float32 [256, 256], replicated, may hold values from -0.1875 to 0.1875
- tile_row: int32 [192, 1], P(('row', 'col')), may hold values from 0 to 7; in each aligned block of 6 rows (0 to 5, 6 to 11, ...) no two rows name the same one
- offsets: int32 [192, 2], P(('row', 'col')), may hold values from 0 to 511
Outputs:
- object_grad: float32 [2, 4096, 2048], P(None, 'row', 'col')
- probe_grad: float32 [3, 2, 256, 256], replicated
The draws below stay inside these ranges and needn't reach their ends.
Inputs may be any that keep to these rules, and one draw needn't show every extreme that they name: `tile_row`: the 6 frames of one device have distinct tile rows.
All inputs are finite; a program needn't handle non-finite values.
Results may differ from the reference program's by a relative error of at most 0.0008.
The reference program's roundings to bfloat16 on the way count: a program that leaves them out, or rounds other values in their place, can miss the bound.
Values may be sent and summed in bfloat16 or wider, within the bound.
A program may use at most 128 MiB of HBM per device.

```python
import math
import jax
import jax.numpy as jnp
import numpy as np
from jax import lax

FRAME = 256
MODES = 3
TILE = 512
FR_DEV = 6
FRAMES = 192
OBJ_ROWS = 4096
OBJ_COLS = 2048
N_ROW = 8
N_COL = 4


def set_ends(entries, rng, low, high):
    place = [jax.random.randint(jax.random.fold_in(rng, axis), (), 0, length) for axis, length in enumerate(entries.shape)]
    longest = entries.shape.index(max(entries.shape))
    next_to = place[:longest] + [(place[longest] + 1) % entries.shape[longest]] + place[longest + 1:]
    return entries.at[tuple(place)].set(low).at[tuple(next_to)].set(high)


def level_of(stream_key, shape, pieces, least, largest):
    def one(axis_at, parts):
        steps = jax.random.uniform(jax.random.fold_in(jax.random.fold_in(stream_key, 6), axis_at), (parts,), jnp.float32, least / len(pieces), largest / len(pieces))
        return jnp.repeat(jnp.exp(steps), shape[axis_at] // parts).reshape((-1,) + (1,) * (len(shape) - axis_at - 1))

    loudness = one(*pieces[0])
    for cut in pieces[1:]:
        loudness = loudness * one(*cut)
    return loudness


def shared_out(key, own, number, rows, count, top, reach, skew):
    sequence = jax.random.permutation(key, count)
    packed, ordinary = shares(count, rows * top, reach, skew, True), shares(count, rows * top, reach, skew, False)
    places = jnp.arange(count)

    def named(lengths, turn):
        used = int((lengths > 0).sum())
        fixed = max(1, used // 4)
        shifted = fixed + (places - fixed + turn * (used - fixed)) % max(1, count - fixed)
        return jnp.zeros((count,), jnp.int32).at[sequence[jnp.where(places < fixed, places, shifted)]].set(jnp.asarray(lengths, jnp.int32))

    lengths = jnp.where(number % 4 == 0, named(packed, number // 4), named(ordinary, number - number // 4 - 1))
    mixed = jax.random.permutation(jax.random.fold_in(own, 3), count)
    giver, sink = mixed[0:count // 2 * 2:2], mixed[1:count // 2 * 2:2]
    margin = jnp.minimum(lengths[giver] - 1, reach - lengths[sink]) // 2
    margin = jnp.where((giver == sequence[0]) | (sink == sequence[0]) | (lengths[sink] == 0), 0, jnp.maximum(margin, 0))
    shifted = jax.random.randint(jax.random.fold_in(own, 4), (count // 2,), 0, 1 << 20) % (margin + 1)
    lengths = lengths.at[giver].add(-shifted).at[sink].add(shifted)
    items = jnp.searchsorted(jnp.cumsum(lengths), jnp.arange(rows * top), side="right").astype(jnp.int32)
    listing = items.reshape(top, rows).T
    listing = listing[jax.random.permutation(jax.random.fold_in(own, 1), rows)]
    turn = jax.random.randint(jax.random.fold_in(own, 2), (rows, 1), 0, top)
    return jnp.take_along_axis(listing, (jnp.arange(top)[None, :] + turn) % top, axis=1)


def shares(number_of, total, most, skew, full):
    loads = [(1 << 20) // math.isqrt(standing ** skew) + 1 for standing in range(1, number_of + 1)]
    largest = most if full else min(most, max(-(-total // number_of), total * loads[0] // sum(loads)))
    least = 1 if total - largest >= number_of - 1 else 0
    counts, surplus = [largest] + [least] * (number_of - 1), total - largest - least * (number_of - 1)
    while surplus > 0:
        movable = [i for i in range(1, number_of) if counts[i] < largest] or [i for i in range(1, number_of) if counts[i] < most]
        pool, budget = sum([loads[i] for i in movable]), surplus
        for i in movable:
            more = min(most - counts[i], max(1, budget * loads[i] // pool), surplus)
            counts[i] = counts[i] + more
            surplus = surplus - more
    return np.array(counts)


def bell_draw(stream_key, extent, width, bound, cuts=(), held_as=jnp.bfloat16):
    values = width * jax.random.normal(stream_key, extent, jnp.float32)
    if cuts:
        values = values * level_of(stream_key, extent, cuts, -0.22, 0.18)
    return jnp.clip(values, -bound, bound).astype(held_as)


def setup_inputs(seed: int = 0) -> dict:
    arg_keys = jax.random.split(jax.random.key(seed), 7)
    object_field = bell_draw(arg_keys[0], (2, OBJ_ROWS, OBJ_COLS), 1.0, 6.0, ((1, 8), (2, 4)), jnp.float32)
    probe = bell_draw(arg_keys[1], (MODES, 2, FRAME, FRAME), 1.0, 6.0, (), jnp.float32)
    raw_counts = jnp.clip(jnp.exp(math.log(10.0) - 4.609084 * jax.random.uniform(arg_keys[2], (FRAMES, FRAME, FRAME), jnp.float32) ** level_of(arg_keys[2], (FRAMES, FRAME, FRAME), ((0, 32),), -0.2, 0.2)), 0.099609375, 10.0).astype(jnp.bfloat16)
    resample_delta = bell_draw(arg_keys[3], (FRAME, FRAME), (4 * FRAME) ** -0.5, 0.1875, (), jnp.float32)
    tile_row_keys = jax.random.split(jax.random.fold_in(arg_keys[4], 1), FRAMES // FR_DEV)
    tile_row_turns = jax.random.permutation(jax.random.fold_in(arg_keys[4], 3), FRAMES // FR_DEV)
    tile_row = jax.vmap(lambda own, number: shared_out(jax.random.fold_in(arg_keys[4], 2), own, number, FR_DEV, N_ROW, 1, 1, 2))(tile_row_keys, tile_row_turns).reshape((FRAMES, 1))
    offsets = set_ends(jax.random.randint(arg_keys[5], (FRAMES, 2), 0, TILE), jax.random.fold_in(arg_keys[5], 1), 0, TILE - 1).astype(jnp.int32)
    return {"object_field": object_field, "probe": probe, "raw_counts": raw_counts, "resample_delta": resample_delta, "tile_row": tile_row, "offsets": offsets}


def product(left, right):
    return jnp.dot(left.astype(jnp.float32), right.astype(jnp.float32), preferred_element_type=jnp.float32)

def dft_tables(points):
    indices = jnp.arange(points, dtype=jnp.int32)
    phases = indices[:, None] * indices[None, :] % points
    angles = phases.astype(jnp.float32) * (2.0 * math.pi / points)
    norming = 1.0 / math.sqrt(points)
    cosine = jnp.cos(angles) * norming
    sine_part = -jnp.sin(angles) * norming
    forward = jnp.concatenate([jnp.concatenate([cosine, -sine_part], 1), jnp.concatenate([sine_part, cosine], 1)], 0)
    backward = jnp.concatenate([jnp.concatenate([cosine, sine_part], 1), jnp.concatenate([-sine_part, cosine], 1)], 0)
    return (forward.astype(jnp.bfloat16), backward.astype(jnp.bfloat16))

def measure(raw_counts, resample_delta):
    points = resample_delta.shape[0]
    resample = (jnp.eye(points, dtype=jnp.float32) + resample_delta).astype(jnp.bfloat16)
    first = jnp.einsum('ij,kjl->kil', resample.astype(jnp.float32), raw_counts.astype(jnp.float32)).astype(jnp.bfloat16)
    second = jnp.einsum('kij,lj->kil', first.astype(jnp.float32), resample.astype(jnp.float32))
    return jnp.sqrt(jnp.maximum(second, 0.0)).astype(jnp.bfloat16)

def frame_terms(window, probe, amplitude, forward, backward):
    mode_count = probe.shape[0]
    points = probe.shape[-1]
    probe_real = probe[:, 0]
    probe_imag = probe[:, 1]
    object_real = window[0]
    object_imag = window[1]
    wave = jnp.stack([probe_real * object_real - probe_imag * object_imag, probe_real * object_imag + probe_imag * object_real], 1)
    wave_cols = wave.transpose(1, 2, 0, 3).reshape(2 * points, mode_count * points).astype(jnp.bfloat16)
    half_done = product(forward, wave_cols).astype(jnp.bfloat16)
    wave_rows = half_done.reshape(2, points, mode_count, points).transpose(2, 1, 0, 3).reshape(mode_count * points, 2 * points)
    far_field = product(wave_rows, backward).reshape(mode_count, points, 2, points)
    intensity = lax.optimization_barrier(jnp.sum(far_field * far_field, axis=(0, 2)))
    scaling = 1.0 - amplitude.astype(jnp.float32) / jnp.sqrt(jnp.maximum(intensity, 1.0))
    residual = (far_field * scaling[None, :, None, :]).astype(jnp.bfloat16).reshape(mode_count * points, 2 * points)
    back_rows = product(residual, forward).astype(jnp.bfloat16)
    back_cols = back_rows.reshape(mode_count, points, 2, points).transpose(2, 1, 0, 3).reshape(2 * points, mode_count * points)
    update = product(backward, back_cols).reshape(2, points, mode_count, points).transpose(2, 0, 1, 3)
    update_real = update[:, 0]
    update_imag = update[:, 1]
    object_term = jnp.stack([lax.optimization_barrier(jnp.sum(probe_real * update_real + probe_imag * update_imag, 0)), lax.optimization_barrier(jnp.sum(probe_real * update_imag - probe_imag * update_real, 0))], 0)
    probe_term = jnp.stack([object_real * update_real + object_imag * update_imag, object_real * update_imag - object_imag * update_real], 1)
    return (object_term, probe_term)

def reference(object_field, probe, raw_counts, resample_delta, tile_row, offsets):
    points = probe.shape[-1]
    half = points // 2
    forward, backward = dft_tables(points)
    amplitudes = measure(raw_counts, resample_delta)
    padded = jnp.pad(object_field, ((0, 0), (half, half), (half, half)))
    frame_ids = jnp.arange(FRAMES, dtype=jnp.int32)
    tile_cols = frame_ids // FR_DEV % N_COL
    tops = (tile_row[:, 0] * TILE + offsets[:, 0]).astype(jnp.int32)
    lefts = (tile_cols * TILE + offsets[:, 1]).astype(jnp.int32)
    anchor = jnp.zeros((), jnp.int32)

    def one_frame(totals, inputs):
        gradient, probe_total = totals
        amplitude, top, left = inputs
        window = lax.dynamic_slice(padded, (anchor, top, left), (2, points, points))
        object_term, probe_term = frame_terms(window, probe, amplitude, forward, backward)
        current = lax.dynamic_slice(gradient, (anchor, top, left), (2, points, points))
        gradient = lax.dynamic_update_slice(gradient, current + object_term, (anchor, top, left))
        return ((gradient, probe_total + probe_term), None)
    start = (jnp.zeros(padded.shape, padded.dtype), jnp.zeros(probe.shape, probe.dtype))
    (gradient, probe_total), _ = lax.scan(one_frame, start, (amplitudes, tops, lefts))
    object_grad = gradient[:, half:half + OBJ_ROWS, half:half + OBJ_COLS]
    probe_grad = probe_total * (1.0 / math.sqrt(FRAMES))
    return (object_grad, probe_grad)
```

```python
import math

import jax
import jax.numpy as jnp
from jax import lax
from jax.experimental import pallas as pl
from jax.experimental.pallas import tpu as pltpu
from jax.sharding import PartitionSpec as P


def extended_2(value, sides, width):
    for axis, dim in sides:
        size, length = (lax.axis_size(axis), value.shape[dim])
        up = [(i, (i + 1) % size) for i in range(size - 1)]
        down = [(j, i) for i, j in up]
        last = lax.slice_in_dim(value, length - width, length, axis=dim)
        first = lax.slice_in_dim(value, 0, width, axis=dim)
        before = lax.ppermute(last, axis, up)
        after = lax.ppermute(first, axis, down)
        value = jnp.concatenate([before, value, after], axis=dim)
    return value


def product(left, right):
    return jnp.dot(left, right, preferred_element_type=jnp.float32)


def dft_tables(points):
    indices = jnp.arange(points, dtype=jnp.int32)
    phases = indices[:, None] * indices[None, :] % points
    angles = phases.astype(jnp.float32) * (2.0 * math.pi / points)
    norming = 1.0 / math.sqrt(points)
    cosine = jnp.cos(angles) * norming
    sine_part = -jnp.sin(angles) * norming
    forward = jnp.concatenate(
        [jnp.concatenate([cosine, -sine_part], 1), jnp.concatenate([sine_part, cosine], 1)], 0
    )
    backward = jnp.concatenate(
        [jnp.concatenate([cosine, sine_part], 1), jnp.concatenate([-sine_part, cosine], 1)], 0
    )
    return (forward.astype(jnp.bfloat16), backward.astype(jnp.bfloat16))


def measure(raw_counts, resample_delta):
    points = resample_delta.shape[0]
    resample = (jnp.eye(points, dtype=jnp.float32) + resample_delta).astype(jnp.bfloat16)
    first = jnp.einsum(
        "ij,kjl->kil", resample, raw_counts, preferred_element_type=jnp.float32
    ).astype(jnp.bfloat16)
    second = jnp.einsum("kij,lj->kil", first, resample, preferred_element_type=jnp.float32)
    return jnp.sqrt(jnp.maximum(second, 0.0)).astype(jnp.bfloat16)


def frames_kernel(
    requests,
    extended,
    probe,
    amplitudes,
    forward,
    backward,
    gradient,
    probe_total,
    window,
    far_field,
):
    mode_count, _, points, _ = probe.shape
    span_rows, span_cols = (points + 8, points + 128)
    gradient[...] = jnp.zeros_like(gradient)
    probe_total[...] = jnp.zeros_like(probe_total)

    def one_slot(slot, carry):
        @pl.when(requests[slot, 2] > 0)
        def _():
            top, left = (requests[slot, 0], requests[slot, 1])
            skip_rows, skip_cols = (lax.rem(top, 8), lax.rem(left, 128))
            rows = pl.ds(pl.multiple_of(top - skip_rows, 8), span_rows)
            cols = pl.ds(pl.multiple_of(left - skip_cols, 128), span_cols)
            for part in range(2):
                block = extended[part, rows, cols]
                block = pltpu.roll(block, lax.rem(span_cols - skip_cols, span_cols), 1)
                block = block[:, :points]
                block = pltpu.roll(block, lax.rem(span_rows - skip_rows, span_rows), 0)
                window[part] = block[:points]
            intensity = jnp.zeros((points, points), jnp.float32)
            for mode in range(mode_count):
                object_real, object_imag = (window[0], window[1])
                probe_real, probe_imag = (probe[mode, 0], probe[mode, 1])
                wave = jnp.concatenate(
                    [
                        (probe_real * object_real - probe_imag * object_imag).astype(jnp.bfloat16),
                        (probe_real * object_imag + probe_imag * object_real).astype(jnp.bfloat16),
                    ],
                    0,
                )
                half_done = product(forward[...], wave).astype(jnp.bfloat16)
                wave_rows = jnp.concatenate([half_done[:points], half_done[points:]], 1)
                field = product(wave_rows, backward[...])
                far_field[mode] = field
                squares = field * field
                intensity = intensity + squares[:, :points] + squares[:, points:]
            amplitude = amplitudes[slot].astype(jnp.float32)
            scaling = 1.0 - amplitude / jnp.sqrt(jnp.maximum(intensity, 1.0))
            scaling = jnp.concatenate([scaling, scaling], 1)
            term_real = jnp.zeros((points, points), jnp.float32)
            term_imag = jnp.zeros((points, points), jnp.float32)
            for mode in range(mode_count):
                residual = (far_field[mode] * scaling).astype(jnp.bfloat16)
                back_rows = product(residual, forward[...]).astype(jnp.bfloat16)
                back_cols = jnp.concatenate([back_rows[:, :points], back_rows[:, points:]], 0)
                update = product(backward[...], back_cols)
                update_real, update_imag = (update[:points], update[points:])
                object_real, object_imag = (window[0], window[1])
                probe_real, probe_imag = (probe[mode, 0], probe[mode, 1])
                term_real = term_real + (probe_real * update_real + probe_imag * update_imag)
                term_imag = term_imag + (probe_real * update_imag - probe_imag * update_real)
                probe_total[mode, 0] += object_real * update_real + object_imag * update_imag
                probe_total[mode, 1] += object_real * update_imag - object_imag * update_real
            for part, term in enumerate((term_real, term_imag)):
                block = jnp.concatenate([term, jnp.zeros((8, points), jnp.float32)], 0)
                block = pltpu.roll(block, skip_rows, 0)
                block = jnp.concatenate([block, jnp.zeros((span_rows, 128), jnp.float32)], 1)
                block = pltpu.roll(block, skip_cols, 1)
                gradient[part, rows, cols] += block

        return carry

    lax.fori_loop(0, requests.shape[0], one_slot, 0)


def frames(requests, extended, probe, amplitudes, forward, backward):
    points = probe.shape[-1]
    vmem = pl.BlockSpec(memory_space=pltpu.VMEM)
    return pl.pallas_call(
        frames_kernel,
        name="frames",
        out_shape=(
            jax.ShapeDtypeStruct(extended.shape, jnp.float32),
            jax.ShapeDtypeStruct(probe.shape, jnp.float32),
        ),
        in_specs=[pl.BlockSpec(memory_space=pltpu.SMEM)] + [vmem] * 5,
        out_specs=(vmem, vmem),
        scratch_shapes=[
            pltpu.VMEM((2, points, points), jnp.float32),
            pltpu.VMEM((probe.shape[0], points, 2 * points), jnp.float32),
        ],
        compiler_params=pltpu.CompilerParams(vmem_limit_bytes=48 * 1024 * 1024),
    )(requests, extended, probe, amplitudes, forward, backward)


def fold(folded, width, tile):
    pieces = ((0, width, 0), (2 * width, tile, 0), (tile + 3 * width, width, tile - width))
    result = jnp.zeros((folded.shape[0], tile, tile), jnp.float32)
    for source_row, length_row, target_row in pieces:
        for source_col, length_col, target_col in pieces:
            block = folded[
                :, source_row : source_row + length_row, source_col : source_col + length_col
            ]
            result = result.at[
                :, target_row : target_row + length_row, target_col : target_col + length_col
            ].add(block)
    return result


def shards(object_field, probe, raw_counts, resample_delta, tile_row, offsets):
    points = probe.shape[-1]
    half = points // 2
    tile = object_field.shape[1]
    tile_rows = lax.axis_size("row")
    frame_total = raw_counts.shape[0] * tile_rows * lax.axis_size("col")
    forward, backward = dft_tables(points)
    amplitudes = measure(raw_counts, resample_delta)
    extended = extended_2(object_field, (("row", 1), ("col", 2)), half)
    slot_ids = jnp.arange(tile_rows, dtype=jnp.int32)
    target = tile_row[:, 0]
    picks = (target[:, None] == slot_ids[None, :]).astype(jnp.int32)
    live = jnp.sum(picks, 0)
    slot_tops = jnp.sum(picks * offsets[:, 0:1], 0)
    slot_lefts = jnp.sum(picks * offsets[:, 1:2], 0)
    requests = jnp.stack([slot_tops, slot_lefts, live], 1)
    outgoing = jnp.einsum(
        "ks,kij->sij", picks.astype(jnp.bfloat16), amplitudes, preferred_element_type=jnp.float32
    ).astype(jnp.bfloat16)
    incoming, received = (
        lax.all_to_all(outgoing, "row", split_axis=0, concat_axis=0, tiled=True),
        lax.all_to_all(requests, "row", split_axis=0, concat_axis=0, tiled=True),
    )

    gradient, probe_total = frames(received, extended, probe, incoming, forward, backward)
    probe_grad = lax.psum(probe_total, ("row", "col")) * (1.0 / math.sqrt(frame_total))
    folded = extended_2(gradient, (("row", 1), ("col", 2)), half)
    object_grad = fold(folded, half, tile)
    return (object_grad, probe_grad)


def solution(mesh):
    placed = (
        P(None, "row", "col"),
        P(),
        P(("row", "col"), None, None),
        P(),
        P(("row", "col"), None),
        P(("row", "col"), None),
    )
    return jax.shard_map(
        shards, mesh=mesh, in_specs=placed, out_specs=(P(None, "row", "col"), P()), check_vma=False
    )
```
